1024 devices in a mesh: dp: 8 (over x, core), chan: 4 (over z_hi), ctx: 32 (over y, z_lo).
Axes of the slice: x: 4, y: 4, z: 32 (z_hi: 4, z_lo: 8; z = z_hi * 8 + z_lo), core: 2. Of those that a mesh axis runs over, the one named last changes fastest.
Arguments:
- query_proj: bfloat16 [8, 4096, 4096], P('dp', 'ctx', 'chan'), may hold values from -6 to 6
- key_proj: bfloat16 [8, 4096, 4096], P('dp', 'ctx', 'chan'), may hold values from -6 to 6
- value_proj: bfloat16 [8, 4096, 4096], P('dp', 'ctx', 'chan'), may hold values from -6 to 6
- out_grad: bfloat16 [8, 4096, 4096], P('dp', 'ctx', 'chan'), may hold values from -6 to 6
- filter_taps: float32 [4096, 4096], P(('chan', 'ctx')), may hold values from -0.09375 to 0.09375
Outputs:
- grad_q: bfloat16 [8, 4096, 4096], P('dp', 'ctx', 'chan')
- grad_k: bfloat16 [8, 4096, 4096], P('dp', 'ctx', 'chan')
- grad_v: bfloat16 [8, 4096, 4096], P('dp', 'ctx', 'chan')
- grad_filt: float32 [4096, 4096], P(('chan', 'ctx'))
The draws below stay inside these ranges and needn't reach their ends.
All inputs are finite; a program needn't handle non-finite values.
Results may differ from the reference program's by a relative error of at most 0.014.
Values may be sent and summed in bfloat16 or wider, within the bound.
A program may use at most 64 MiB of HBM per device.

```python
import math
import jax
import jax.numpy as jnp
from jax import lax

D = 4096
SEQS = 8
L = 4096


def level_of(key, extent, shards, smallest, high):
    gain = 1.0
    for dim, shards_of in shards:
        draws = jax.random.uniform(jax.random.fold_in(jax.random.fold_in(key, 6), dim), (shards_of,), jnp.float32, smallest / len(shards), high / len(shards))
        gain = gain * jnp.repeat(jnp.exp(draws), extent[dim] // shards_of).reshape((-1,) + (1,) * (len(extent) - 1 - dim))
    return gain


def gaussian(stream_key, shape, scale, most, pieces=(), held_as=jnp.bfloat16):
    entries = jax.random.normal(stream_key, shape, jnp.float32) * scale
    if len(pieces) > 0:
        entries = level_of(stream_key, shape, pieces, -0.22, 0.18) * entries
    return jnp.clip(entries, min=-most, max=most).astype(held_as)


def setup_inputs(seed: int = 0) -> dict:
    keys = jax.random.split(jax.random.key(seed), 6)
    query_proj = gaussian(keys[0], (SEQS, L, D), 1.0, 6.0, ((0, 8), (1, 32), (2, 4)))
    key_proj = gaussian(keys[1], (SEQS, L, D), 1.0, 6.0, ((0, 8), (1, 32), (2, 4)))
    value_proj = gaussian(keys[2], (SEQS, L, D), 1.0, 6.0, ((0, 8), (1, 32), (2, 4)))
    out_grad = gaussian(keys[3], (SEQS, L, D), 1.0, 6.0, ((0, 8), (1, 32), (2, 4)))
    filter_taps = gaussian(keys[4], (D, L), L ** -0.5, 0.09375, ((0, 128),), jnp.float32)
    return {"query_proj": query_proj, "key_proj": key_proj, "value_proj": value_proj, "out_grad": out_grad, "filter_taps": filter_taps}


def channel_block(inputs):
    gated_blk, grad_blk, taps_blk = inputs
    length = taps_blk.shape[1]
    padded = 2 * length
    gate_spec = jnp.fft.rfft(gated_blk.astype(jnp.float32), n=padded, axis=1)
    grad_spec = jnp.fft.rfft(grad_blk.astype(jnp.float32), n=padded, axis=1)
    filt_spec = jnp.fft.rfft(taps_blk.astype(jnp.float32), n=padded, axis=1).T[None]
    conv_out = jnp.fft.irfft(gate_spec * filt_spec, n=padded, axis=1)[:, :length].astype(jnp.bfloat16)
    back_conv = jnp.fft.irfft(grad_spec * jnp.conj(filt_spec), n=padded, axis=1)[:, :length].astype(jnp.bfloat16)
    cross_corr = jnp.fft.irfft(jnp.conj(gate_spec) * grad_spec, n=padded, axis=1)[:, :length]
    return conv_out, back_conv, jnp.sum(cross_corr, axis=0).T


def reference(query_proj, key_proj, value_proj, out_grad, filter_taps):
    seq_count, length, channels = query_proj.shape
    block_size = math.gcd(channels, 512)
    block_count = channels // block_size
    query_vals = query_proj.astype(jnp.float32)
    key_vals = key_proj.astype(jnp.float32)
    grad_vals = out_grad.astype(jnp.float32)
    gated = (query_vals * key_vals).astype(jnp.bfloat16)
    grad_conv = (grad_vals * value_proj.astype(jnp.float32)).astype(jnp.bfloat16)

    def split_blocks(values):
        return values.reshape(seq_count, length, block_count, block_size).transpose(2, 0, 1, 3)

    def join_blocks(values):
        return values.transpose(1, 2, 0, 3).reshape(seq_count, length, channels)

    conv_out, back_conv, grad_filt = lax.map(
        channel_block,
        (split_blocks(gated), split_blocks(grad_conv), filter_taps.reshape(block_count, block_size, length)))
    conv_out = join_blocks(conv_out)
    back_vals = join_blocks(back_conv).astype(jnp.float32)
    grad_q = (back_vals * key_vals).astype(jnp.bfloat16)
    grad_k = (back_vals * query_vals).astype(jnp.bfloat16)
    grad_v = (grad_vals * conv_out.astype(jnp.float32)).astype(jnp.bfloat16)
    return grad_q, grad_k, grad_v, grad_filt.reshape(channels, length)
```

```python
import functools
import math

import jax
import jax.numpy as jnp
import ml_dtypes
import numpy as np
from jax import lax
from jax.experimental import pallas as pl
from jax.experimental.pallas import tpu as pltpu
from jax.sharding import PartitionSpec as P

MESH = pl.DeviceIdType.MESH
ROWS = 16
COLS = 128
F32 = jnp.float32
BF16 = jnp.bfloat16


def make_tables(blocks):
    freq = np.arange(blocks) + 0.5
    outer = np.exp(-2j * np.pi * np.outer(freq, np.arange(blocks)) / (2 * blocks))
    eye = np.eye(ROWS)
    spread = lambda table: np.kron(table, eye)
    outer_fwd = np.concatenate([spread(outer.real), spread(outer.imag)], axis=0)
    length = 2 * blocks * COLS
    back = outer.conj().T * (2.0 / length)
    outer_inv = np.concatenate([spread(back.real), spread(-back.imag)], axis=1)
    inner = np.exp(-2j * np.pi * np.outer(np.arange(COLS), np.arange(COLS)) / COLS)
    inner_fwd = np.block([[inner.real, inner.imag], [-inner.imag, inner.real]])
    inner_inv = np.block([[inner.real, -inner.imag], [inner.imag, inner.real]])
    twist = np.exp(-2j * np.pi * np.outer(freq, np.arange(COLS)) / length)
    twist = np.repeat(twist, ROWS, axis=0)
    half = lambda table: np.asarray(table).astype(ml_dtypes.bfloat16)
    full = lambda table: np.asarray(table).astype(np.float32)
    return (half(outer_fwd), half(outer_inv), half(inner_fwd), half(inner_inv), full(twist.real), full(twist.imag))


def dot(left, right):
    return jnp.dot(left, right, preferred_element_type=F32)


def kernel(
    blocks, parts, cols,
    query_ref, key_ref, value_ref, grad_ref, taps_ref,
    outer_fwd, outer_inv, inner_fwd, inner_inv, twist_re, twist_im,
    conv_out, back_out, filt_out,
    send_buf, recv_buf, ret_send, ret_recv,
    filt_re, filt_im, cross_rows, cross_buf, part_buf, sum_buf, full_buf,
    send_sem, recv_sem, ret_send_sem, ret_recv_sem, own_sem, red_send, red_recv, all_send, all_recv,
):
    me = lax.axis_index("ctx")
    mine = lax.axis_index("dp")
    lines = blocks // cols
    row_at, col_at = me // cols, me % cols
    span = blocks * ROWS
    group = COLS // (2 * ROWS)
    piece = blocks // parts

    def peer(step):
        turn = step // lines
        shift = cols // 2 + ((turn + 1) // 2) * (1 - 2 * (turn % 2))
        down = (step % lines + 1) % lines
        return ((row_at + down) % lines) * cols + (col_at + shift) % cols

    barrier = pltpu.get_barrier_semaphore()

    def greet(step, carry):
        pl.semaphore_signal(barrier, inc=1, device_id={"ctx": peer(step)}, device_id_type=MESH)
        return carry

    def greet_part(step, carry):
        pl.semaphore_signal(barrier, inc=1, device_id={"dp": (mine + 1 + step) % parts}, device_id_type=MESH)
        return carry

    lax.fori_loop(0, blocks - 1, greet, 0)
    lax.fori_loop(0, parts - 1, greet_part, 0)

    for number, (left_ref, right_ref) in enumerate(((query_ref, key_ref), (grad_ref, value_ref))):
        for block in range(blocks // group):
            lanes = slice(block * COLS, (block + 1) * COLS)
            product = left_ref[:, lanes].astype(F32) * right_ref[:, lanes].astype(F32)
            turned = product.T.astype(BF16).reshape(group, 2, ROWS, COLS)
            for half in range(2):
                send_buf[half, number, block * group:(block + 1) * group] = turned[:, half]

    pl.semaphore_wait(barrier, blocks - 1 + parts - 1)

    def send_tokens(half):
        def start(step, carry):
            dest = peer(step)
            pltpu.make_async_remote_copy(
                src_ref=send_buf.at[half, :, dest], dst_ref=recv_buf.at[half, :, me],
                send_sem=send_sem.at[half], recv_sem=recv_sem.at[half],
                device_id={"ctx": dest}, device_id_type=MESH,
            ).start()
            return carry

        lax.fori_loop(0, blocks - 1, start, 0)

    def send_back(half):
        def start(step, carry):
            dest = peer(step)
            pltpu.make_async_remote_copy(
                src_ref=ret_send.at[half, :, dest], dst_ref=ret_recv.at[half, :, me],
                send_sem=ret_send_sem.at[half], recv_sem=ret_recv_sem.at[half],
                device_id={"ctx": dest}, device_id_type=MESH,
            ).start()
            return carry

        lax.fori_loop(0, blocks - 1, start, 0)

    def wait_bytes(ref, sem):
        pltpu.make_async_copy(ref, ref, sem).wait()

    def others(ref, half):
        return ref.at[half, :, pl.ds(0, blocks - 1)]

    def own_copy(half):
        return pltpu.make_async_copy(send_buf.at[half, :, me], recv_buf.at[half, :, me], own_sem.at[half])

    def own_back(half):
        return pltpu.make_async_copy(ret_send.at[half, :, me], ret_recv.at[half, :, me], own_sem.at[2 + half])

    for half in range(2):
        send_tokens(half)
    for half in range(2):
        own_copy(half).start()

    def forward(rows):
        first = dot(outer_fwd[...], rows)
        spectra = []
        for block in range(2):
            lanes = slice(block * COLS, (block + 1) * COLS)
            real, imag = first[:span, lanes], first[span:, lanes]
            turned_re = real * twist_re[...] - imag * twist_im[...]
            turned_im = real * twist_im[...] + imag * twist_re[...]
            both = jnp.concatenate([turned_re.astype(BF16), turned_im.astype(BF16)], axis=1)
            result = dot(both, inner_fwd[...])
            spectra.append((result[:, :COLS], result[:, COLS:]))
        return spectra

    def inverse_inner(real, imag):
        both = jnp.concatenate([real.astype(BF16), imag.astype(BF16)], axis=1)
        result = dot(both, inner_inv[...])
        real, imag = result[:, :COLS], result[:, COLS:]
        turned_re = real * twist_re[...] + imag * twist_im[...]
        turned_im = imag * twist_re[...] - real * twist_im[...]
        return jnp.concatenate([turned_re.astype(BF16), turned_im.astype(BF16)], axis=0)

    taps_rows = jnp.concatenate(
        [
            jnp.concatenate(
                [taps_ref[half * ROWS:(half + 1) * ROWS, a * COLS:(a + 1) * COLS] for a in range(blocks)], axis=0
            ).astype(BF16)
            for half in range(2)
        ],
        axis=1,
    )
    for half, (real, imag) in enumerate(forward(taps_rows)):
        filt_re[half] = real
        filt_im[half] = imag

    for half in range(2):
        wait_bytes(others(recv_buf, half), recv_sem.at[half])
        own_copy(half).wait()
        rows = jnp.concatenate(
            [recv_buf[half, 0].reshape(span, COLS), recv_buf[half, 1].reshape(span, COLS)], axis=1
        )
        (gate_re, gate_im), (grad_re, grad_im) = forward(rows)
        tap_re, tap_im = filt_re[half], filt_im[half]
        conv = inverse_inner(gate_re * tap_re - gate_im * tap_im, gate_re * tap_im + gate_im * tap_re)
        back = inverse_inner(grad_re * tap_re + grad_im * tap_im, grad_im * tap_re - grad_re * tap_im)
        result = dot(outer_inv[...], jnp.concatenate([conv, back], axis=1)).astype(BF16)
        ret_send[half, 0] = result[:, :COLS].reshape(blocks, ROWS, COLS)
        ret_send[half, 1] = result[:, COLS:].reshape(blocks, ROWS, COLS)
        send_back(half)
        own_back(half).start()
        cross_rows[half] = inverse_inner(gate_re * grad_re + gate_im * grad_im, gate_re * grad_im - gate_im * grad_re)

    cross = dot(outer_inv[...], jnp.concatenate([cross_rows[0], cross_rows[1]], axis=1)).astype(BF16)
    for half in range(2):
        cross_buf[:, half * ROWS:(half + 1) * ROWS] = cross[:, half * COLS:(half + 1) * COLS].reshape(blocks, ROWS, COLS)

    def start_part(step, carry):
        dest = (mine + 1 + step) % parts
        pltpu.make_async_remote_copy(
            src_ref=cross_buf.at[pl.ds(dest * piece, piece)], dst_ref=part_buf.at[mine],
            send_sem=red_send.at[0], recv_sem=red_recv.at[0], device_id={"dp": dest}, device_id_type=MESH,
        ).start()
        return carry

    lax.fori_loop(0, parts - 1, start_part, 0)
    own_part = pltpu.make_async_copy(cross_buf.at[pl.ds(mine * piece, piece)], part_buf.at[mine], own_sem.at[4])
    own_part.start()
    wait_bytes(part_buf.at[pl.ds(0, parts - 1)], red_recv.at[0])
    own_part.wait()
    total = part_buf[0].astype(F32)
    for part in range(1, parts):
        total = total + part_buf[part].astype(F32)
    sum_buf[...] = total.astype(BF16)

    def start_sum(step, carry):
        dest = (mine + 1 + step) % parts
        pltpu.make_async_remote_copy(
            src_ref=sum_buf, dst_ref=full_buf.at[mine],
            send_sem=all_send.at[0], recv_sem=all_recv.at[0], device_id={"dp": dest}, device_id_type=MESH,
        ).start()
        return carry

    lax.fori_loop(0, parts - 1, start_sum, 0)
    own_sum = pltpu.make_async_copy(sum_buf, full_buf.at[mine], own_sem.at[5])
    own_sum.start()
    wait_bytes(full_buf.at[pl.ds(0, parts - 1)], all_recv.at[0])
    own_sum.wait()
    for a in range(blocks):
        filt_out[:, a * COLS:(a + 1) * COLS] = full_buf[a // piece, a % piece].astype(filt_out.dtype)

    for half in range(2):
        wait_bytes(others(ret_recv, half), ret_recv_sem.at[half])
        own_back(half).wait()
    for number, out_ref in enumerate((conv_out, back_out)):
        for block in range(blocks // group):
            owners = slice(block * group, (block + 1) * group)
            rows = jnp.stack([ret_recv[0, number, owners], ret_recv[1, number, owners]], axis=1)
            out_ref[:, block * COLS:(block + 1) * COLS] = rows.reshape(COLS, COLS).astype(F32).T.astype(BF16)

    for half in range(2):
        wait_bytes(others(send_buf, half), send_sem.at[half])
        wait_bytes(others(ret_send, half), ret_send_sem.at[half])
    wait_bytes(part_buf.at[pl.ds(0, parts - 1)], red_send.at[0])
    wait_bytes(full_buf.at[pl.ds(0, parts - 1)], all_send.at[0])


def local(blocks, parts, cols, query_proj, key_proj, value_proj, out_grad, filter_taps):
    tokens, channels = query_proj.shape[1:]
    tables = make_tables(blocks)
    span = blocks * ROWS
    piece = blocks // parts
    messages = (2, 2, blocks, ROWS, COLS)
    vmem = pl.BlockSpec(memory_space=pltpu.VMEM)
    conv_local, back_local, filt_sum = pl.pallas_call(
        functools.partial(kernel, blocks, parts, cols),
        out_shape=(
            jax.ShapeDtypeStruct((tokens, channels), BF16),
            jax.ShapeDtypeStruct((tokens, channels), BF16),
            jax.ShapeDtypeStruct(filter_taps.shape, BF16),
        ),
        in_specs=[vmem] * 11,
        out_specs=(vmem,) * 3,
        scratch_shapes=[
            pltpu.VMEM(messages, BF16),
            pltpu.VMEM(messages, BF16),
            pltpu.VMEM(messages, BF16),
            pltpu.VMEM(messages, BF16),
            pltpu.VMEM((2, span, COLS), F32),
            pltpu.VMEM((2, span, COLS), F32),
            pltpu.VMEM((2, 2 * span, COLS), BF16),
            pltpu.VMEM((blocks, 2 * ROWS, COLS), BF16),
            pltpu.VMEM((parts, piece, 2 * ROWS, COLS), BF16),
            pltpu.VMEM((piece, 2 * ROWS, COLS), BF16),
            pltpu.VMEM((parts, piece, 2 * ROWS, COLS), BF16),
            pltpu.SemaphoreType.DMA((2,)),
            pltpu.SemaphoreType.DMA((2,)),
            pltpu.SemaphoreType.DMA((2,)),
            pltpu.SemaphoreType.DMA((2,)),
            pltpu.SemaphoreType.DMA((6,)),
            pltpu.SemaphoreType.DMA((1,)),
            pltpu.SemaphoreType.DMA((1,)),
            pltpu.SemaphoreType.DMA((1,)),
            pltpu.SemaphoreType.DMA((1,)),
        ],
        compiler_params=pltpu.CompilerParams(
            collective_id=0, has_side_effects=True, vmem_limit_bytes=56 * 2**20
        ),
    )(query_proj[0], key_proj[0], value_proj[0], out_grad[0], filter_taps, *map(jnp.asarray, tables))
    back_vals = back_local.astype(F32)
    grad_q = (back_vals * key_proj[0].astype(F32)).astype(BF16)[None]
    grad_k = (back_vals * query_proj[0].astype(F32)).astype(BF16)[None]
    grad_v = (out_grad[0].astype(F32) * conv_local.astype(F32)).astype(BF16)[None]
    return grad_q, grad_k, grad_v, filt_sum.astype(F32)


def solution(mesh):
    blocks, parts = mesh.shape["ctx"], mesh.shape["dp"]
    cols = max(blocks // 4, 1)
    tokens = P("dp", "ctx", "chan")
    filt = P(("chan", "ctx"), None)
    return jax.shard_map(
        functools.partial(local, blocks, parts, cols),
        mesh=mesh,
        in_specs=(tokens, tokens, tokens, tokens, filt),
        out_specs=(tokens, tokens, tokens, filt),
        check_vma=False,
    )
```

```python
import functools
import math

import jax
import jax.numpy as jnp
import ml_dtypes
import numpy as np
from jax import lax
from jax.experimental import pallas as pl
from jax.experimental.pallas import tpu as pltpu
from jax.sharding import PartitionSpec as P

MESH = pl.DeviceIdType.MESH
ROWS = 16
COLS = 128
F32 = jnp.float32
BF16 = jnp.bfloat16


def make_tables(blocks):
    freq = np.arange(blocks) + 0.5
    outer = np.exp(-2j * np.pi * np.outer(freq, np.arange(blocks)) / (2 * blocks))
    eye = np.eye(ROWS)
    spread = lambda table: np.kron(table, eye)
    outer_fwd = np.concatenate([spread(outer.real), spread(outer.imag)], axis=0)
    length = 2 * blocks * COLS
    back = outer.conj().T * (2.0 / length)
    outer_inv = np.concatenate([spread(back.real), spread(-back.imag)], axis=1)
    inner = np.exp(-2j * np.pi * np.outer(np.arange(COLS), np.arange(COLS)) / COLS)
    inner_fwd = np.block([[inner.real, inner.imag], [-inner.imag, inner.real]])
    inner_inv = np.block([[inner.real, -inner.imag], [inner.imag, inner.real]])
    twist = np.exp(-2j * np.pi * np.outer(freq, np.arange(COLS)) / length)
    twist = np.repeat(twist, ROWS, axis=0)
    half = lambda table: np.asarray(table).astype(ml_dtypes.bfloat16)
    full = lambda table: np.asarray(table).astype(np.float32)
    return (half(outer_fwd), half(outer_inv), half(inner_fwd), half(inner_inv), full(twist.real), full(twist.imag))


def dot(left, right):
    return jnp.dot(left, right, preferred_element_type=F32)


def kernel(
    blocks, parts, cols,
    query_hbm, key_hbm, value_hbm, grad_hbm, taps_hbm,
    outer_fwd_hbm, outer_inv_hbm, inner_fwd_hbm, inner_inv_hbm, twist_re_hbm, twist_im_hbm,
    conv_out, back_out, filt_out,
    query_ref, key_ref, value_ref, grad_ref, taps_ref,
    outer_fwd, outer_inv, inner_fwd, inner_inv, twist_re, twist_im,
    send_buf, recv_buf, ret_send, ret_recv,
    filt_re, filt_im, cross_buf, part_buf, sum_buf, full_buf,
    send_sem, recv_sem, ret_send_sem, ret_recv_sem, own_sem, load_sem, red_send, red_recv, all_send, all_recv,
):
    me = lax.axis_index("ctx")
    mine = lax.axis_index("dp")
    lines = blocks // cols
    row_at, col_at = me // cols, me % cols
    span = blocks * ROWS
    group = COLS // (2 * ROWS)
    piece = blocks // parts

    def peer(step):
        turn = step // lines
        shift = cols // 2 + ((turn + 1) // 2) * (1 - 2 * (turn % 2))
        down = (step % lines + 1) % lines
        return ((row_at + down) % lines) * cols + (col_at + shift) % cols

    barrier = pltpu.get_barrier_semaphore()

    def greet(step, carry):
        pl.semaphore_signal(barrier, inc=1, device_id={"ctx": peer(step)}, device_id_type=MESH)
        return carry

    def greet_part(step, carry):
        pl.semaphore_signal(barrier, inc=1, device_id={"dp": (mine + 1 + step) % parts}, device_id_type=MESH)
        return carry

    lax.fori_loop(0, blocks - 1, greet, 0)
    lax.fori_loop(0, parts - 1, greet_part, 0)

    loads = [
        pltpu.make_async_copy(source, target, load_sem.at[number])
        for number, (source, target) in enumerate(
            (
                (query_hbm, query_ref), (key_hbm, key_ref), (grad_hbm, grad_ref), (value_hbm, value_ref),
                (taps_hbm, taps_ref), (outer_fwd_hbm, outer_fwd), (inner_fwd_hbm, inner_fwd),
                (twist_re_hbm, twist_re), (twist_im_hbm, twist_im),
                (outer_inv_hbm, outer_inv), (inner_inv_hbm, inner_inv),
            )
        )
    ]
    for load in loads:
        load.start()
    for number, (left_ref, right_ref) in enumerate(((query_ref, key_ref), (grad_ref, value_ref))):
        loads[2 * number].wait()
        loads[2 * number + 1].wait()
        for block in range(blocks // group):
            lanes = slice(block * COLS, (block + 1) * COLS)
            product = left_ref[:, lanes].astype(F32) * right_ref[:, lanes].astype(F32)
            turned = product.T.astype(BF16).reshape(group, 2, ROWS, COLS)
            for half in range(2):
                send_buf[half, number, block * group:(block + 1) * group] = turned[:, half]

    pl.semaphore_wait(barrier, blocks - 1 + parts - 1)

    def send_tokens(half):
        def start(step, carry):
            dest = peer(step)
            pltpu.make_async_remote_copy(
                src_ref=send_buf.at[half, :, dest], dst_ref=recv_buf.at[half, :, me],
                send_sem=send_sem.at[half], recv_sem=recv_sem.at[half],
                device_id={"ctx": dest}, device_id_type=MESH,
            ).start()
            return carry

        lax.fori_loop(0, blocks - 1, start, 0)

    def send_back(half):
        def start(step, carry):
            dest = peer(step)
            pltpu.make_async_remote_copy(
                src_ref=ret_send.at[half, :, dest], dst_ref=ret_recv.at[half, :, me],
                send_sem=ret_send_sem.at[half], recv_sem=ret_recv_sem.at[half],
                device_id={"ctx": dest}, device_id_type=MESH,
            ).start()
            return carry

        lax.fori_loop(0, blocks - 1, start, 0)

    def wait_bytes(ref, sem):
        pltpu.make_async_copy(ref, ref, sem).wait()

    def others(ref, half):
        return ref.at[half, :, pl.ds(0, blocks - 1)]

    def own_copy(half):
        return pltpu.make_async_copy(send_buf.at[half, :, me], recv_buf.at[half, :, me], own_sem.at[half])

    def own_back(half):
        return pltpu.make_async_copy(ret_send.at[half, :, me], ret_recv.at[half, :, me], own_sem.at[2 + half])

    for half in range(2):
        send_tokens(half)
    for half in range(2):
        own_copy(half).start()

    def forward(rows):
        first = dot(outer_fwd[...], rows)
        spectra = []
        for block in range(2):
            lanes = slice(block * COLS, (block + 1) * COLS)
            real, imag = first[:span, lanes], first[span:, lanes]
            turned_re = real * twist_re[...] - imag * twist_im[...]
            turned_im = real * twist_im[...] + imag * twist_re[...]
            both = jnp.concatenate([turned_re.astype(BF16), turned_im.astype(BF16)], axis=1)
            result = dot(both, inner_fwd[...])
            spectra.append((result[:, :COLS], result[:, COLS:]))
        return spectra

    def inverse_inner(real, imag):
        both = jnp.concatenate([real.astype(BF16), imag.astype(BF16)], axis=1)
        result = dot(both, inner_inv[...])
        real, imag = result[:, :COLS], result[:, COLS:]
        turned_re = real * twist_re[...] + imag * twist_im[...]
        turned_im = imag * twist_re[...] - real * twist_im[...]
        return jnp.concatenate([turned_re.astype(BF16), turned_im.astype(BF16)], axis=0)

    for load in loads[4:]:
        load.wait()
    taps_rows = jnp.concatenate(
        [
            jnp.concatenate(
                [taps_ref[half * ROWS:(half + 1) * ROWS, a * COLS:(a + 1) * COLS] for a in range(blocks)], axis=0
            ).astype(BF16)
            for half in range(2)
        ],
        axis=1,
    )
    for half, (real, imag) in enumerate(forward(taps_rows)):
        filt_re[half] = real
        filt_im[half] = imag

    def start_part(half):
        def start(step, carry):
            dest = (mine + 1 + step) % parts
            pltpu.make_async_remote_copy(
                src_ref=cross_buf.at[half, pl.ds(dest * piece, piece)], dst_ref=part_buf.at[half, mine],
                send_sem=red_send.at[half], recv_sem=red_recv.at[half], device_id={"dp": dest}, device_id_type=MESH,
            ).start()
            return carry

        lax.fori_loop(0, parts - 1, start, 0)

    def own_part(half):
        return pltpu.make_async_copy(
            cross_buf.at[half, pl.ds(mine * piece, piece)], part_buf.at[half, mine], own_sem.at[4 + half]
        )

    def start_sum(half):
        def start(step, carry):
            dest = (mine + 1 + step) % parts
            pltpu.make_async_remote_copy(
                src_ref=sum_buf.at[half], dst_ref=full_buf.at[half, mine],
                send_sem=all_send.at[half], recv_sem=all_recv.at[half], device_id={"dp": dest}, device_id_type=MESH,
            ).start()
            return carry

        lax.fori_loop(0, parts - 1, start, 0)

    def own_sum(half):
        return pltpu.make_async_copy(sum_buf.at[half], full_buf.at[half, mine], own_sem.at[6 + half])

    def add_parts(half):
        wait_bytes(part_buf.at[half, pl.ds(0, parts - 1)], red_recv.at[half])
        own_part(half).wait()
        total = part_buf[half, 0].astype(F32)
        for part in range(1, parts):
            total = total + part_buf[half, part].astype(F32)
        sum_buf[half] = total.astype(BF16)
        start_sum(half)
        own_sum(half).start()

    for half in range(2):
        if half == 1:
            add_parts(0)
        wait_bytes(others(recv_buf, half), recv_sem.at[half])
        own_copy(half).wait()
        rows = jnp.concatenate(
            [recv_buf[half, 0].reshape(span, COLS), recv_buf[half, 1].reshape(span, COLS)], axis=1
        )
        (gate_re, gate_im), (grad_re, grad_im) = forward(rows)
        tap_re, tap_im = filt_re[half], filt_im[half]
        conv = inverse_inner(gate_re * tap_re - gate_im * tap_im, gate_re * tap_im + gate_im * tap_re)
        back = inverse_inner(grad_re * tap_re + grad_im * tap_im, grad_im * tap_re - grad_re * tap_im)
        result = dot(outer_inv[...], jnp.concatenate([conv, back], axis=1)).astype(BF16)
        ret_send[half, 0] = result[:, :COLS].reshape(blocks, ROWS, COLS)
        ret_send[half, 1] = result[:, COLS:].reshape(blocks, ROWS, COLS)
        send_back(half)
        own_back(half).start()
        cross = inverse_inner(gate_re * grad_re + gate_im * grad_im, gate_re * grad_im - gate_im * grad_re)
        cross_buf[half] = dot(outer_inv[...], cross).astype(BF16).reshape(blocks, ROWS, COLS)
        start_part(half)
        own_part(half).start()

    add_parts(1)
    for half in range(2):
        wait_bytes(full_buf.at[half, pl.ds(0, parts - 1)], all_recv.at[half])
        own_sum(half).wait()
        for a in range(blocks):
            lanes = slice(a * COLS, (a + 1) * COLS)
            filt_out[half * ROWS:(half + 1) * ROWS, lanes] = full_buf[half, a // piece, a % piece]

    for half in range(2):
        wait_bytes(others(ret_recv, half), ret_recv_sem.at[half])
        own_back(half).wait()
    for number, out_ref in enumerate((conv_out, back_out)):
        for block in range(blocks // group):
            owners = slice(block * group, (block + 1) * group)
            rows = jnp.stack([ret_recv[0, number, owners], ret_recv[1, number, owners]], axis=1)
            out_ref[:, block * COLS:(block + 1) * COLS] = rows.reshape(COLS, COLS).astype(F32).T.astype(BF16)

    for half in range(2):
        wait_bytes(others(send_buf, half), send_sem.at[half])
        wait_bytes(others(ret_send, half), ret_send_sem.at[half])
        wait_bytes(part_buf.at[half, pl.ds(0, parts - 1)], red_send.at[half])
        wait_bytes(full_buf.at[half, pl.ds(0, parts - 1)], all_send.at[half])


def local(blocks, parts, cols, query_proj, key_proj, value_proj, out_grad, filter_taps):
    tokens, channels = query_proj.shape[1:]
    tables = make_tables(blocks)
    span = blocks * ROWS
    piece = blocks // parts
    messages = (2, 2, blocks, ROWS, COLS)
    vmem = pl.BlockSpec(memory_space=pltpu.VMEM)
    hbm = pl.BlockSpec(memory_space=pltpu.HBM)
    operands = (query_proj[0], key_proj[0], value_proj[0], out_grad[0], filter_taps, *map(jnp.asarray, tables))
    operands = tuple(pltpu.with_memory_space_constraint(operand, pltpu.HBM) for operand in operands)
    conv_local, back_local, filt_sum = pl.pallas_call(
        functools.partial(kernel, blocks, parts, cols),
        out_shape=(
            jax.ShapeDtypeStruct((tokens, channels), BF16),
            jax.ShapeDtypeStruct((tokens, channels), BF16),
            jax.ShapeDtypeStruct(filter_taps.shape, BF16),
        ),
        in_specs=[hbm] * 11,
        out_specs=(vmem,) * 3,
        scratch_shapes=[
            *(pltpu.VMEM(operand.shape, operand.dtype) for operand in operands),
            pltpu.VMEM(messages, BF16),
            pltpu.VMEM(messages, BF16),
            pltpu.VMEM(messages, BF16),
            pltpu.VMEM(messages, BF16),
            pltpu.VMEM((2, span, COLS), F32),
            pltpu.VMEM((2, span, COLS), F32),
            pltpu.VMEM((2, blocks, ROWS, COLS), BF16),
            pltpu.VMEM((2, parts, piece, ROWS, COLS), BF16),
            pltpu.VMEM((2, piece, ROWS, COLS), BF16),
            pltpu.VMEM((2, parts, piece, ROWS, COLS), BF16),
            pltpu.SemaphoreType.DMA((2,)),
            pltpu.SemaphoreType.DMA((2,)),
            pltpu.SemaphoreType.DMA((2,)),
            pltpu.SemaphoreType.DMA((2,)),
            pltpu.SemaphoreType.DMA((8,)),
            pltpu.SemaphoreType.DMA((11,)),
            pltpu.SemaphoreType.DMA((2,)),
            pltpu.SemaphoreType.DMA((2,)),
            pltpu.SemaphoreType.DMA((2,)),
            pltpu.SemaphoreType.DMA((2,)),
        ],
        compiler_params=pltpu.CompilerParams(
            collective_id=0, has_side_effects=True, vmem_limit_bytes=24 * 2**20
        ),
    )(*operands)
    back_vals = back_local.astype(F32)
    grad_q = (back_vals * key_proj[0].astype(F32)).astype(BF16)[None]
    grad_k = (back_vals * query_proj[0].astype(F32)).astype(BF16)[None]
    grad_v = (out_grad[0].astype(F32) * conv_local.astype(F32)).astype(BF16)[None]
    return grad_q, grad_k, grad_v, filt_sum.astype(F32)


def solution(mesh):
    blocks, parts = mesh.shape["ctx"], mesh.shape["dp"]
    cols = max(blocks // 4, 1)
    tokens = P("dp", "ctx", "chan")
    filt = P(("chan", "ctx"), None)
    return jax.shard_map(
        functools.partial(local, blocks, parts, cols),
        mesh=mesh,
        in_specs=(tokens, tokens, tokens, tokens, filt),
        out_specs=(tokens, tokens, tokens, filt),
        check_vma=False,
    )
```

```python
import functools
import math

import jax
import jax.numpy as jnp
import ml_dtypes
import numpy as np
from jax import lax
from jax.experimental import pallas as pl
from jax.experimental.pallas import tpu as pltpu
from jax.sharding import PartitionSpec as P

MESH = pl.DeviceIdType.MESH
ROWS = 16
COLS = 128
F32 = jnp.float32
BF16 = jnp.bfloat16


def make_tables(blocks):
    freq = np.arange(blocks) + 0.5
    outer = np.exp(-2j * np.pi * np.outer(freq, np.arange(blocks)) / (2 * blocks))
    eye = np.eye(ROWS)
    spread = lambda table: np.kron(table, eye)
    outer_fwd = np.concatenate([spread(outer.real), spread(outer.imag)], axis=0)
    length = 2 * blocks * COLS
    back = outer.conj().T * (2.0 / length)
    outer_inv = np.concatenate([spread(back.real), spread(-back.imag)], axis=1)
    inner = np.exp(-2j * np.pi * np.outer(np.arange(COLS), np.arange(COLS)) / COLS)
    inner_fwd = np.block([[inner.real, inner.imag], [-inner.imag, inner.real]])
    inner_inv = np.block([[inner.real, -inner.imag], [inner.imag, inner.real]])
    twist = np.exp(-2j * np.pi * np.outer(freq, np.arange(COLS)) / length)
    twist = np.repeat(twist, ROWS, axis=0)
    half = lambda table: np.asarray(table).astype(ml_dtypes.bfloat16)
    full = lambda table: np.asarray(table).astype(np.float32)
    return (half(outer_fwd), half(outer_inv), half(inner_fwd), half(inner_inv), full(twist.real), full(twist.imag))


def dot(left, right):
    return jnp.dot(left, right, preferred_element_type=F32)


def kernel(
    blocks, parts, cols,
    query_hbm, key_hbm, value_hbm, grad_hbm, taps_hbm,
    outer_fwd_hbm, outer_inv_hbm, inner_fwd_hbm, inner_inv_hbm, twist_re_hbm, twist_im_hbm,
    conv_out, back_out, filt_out,
    query_ref, key_ref, value_ref, grad_ref, taps_ref,
    outer_fwd, outer_inv, inner_fwd, inner_inv, twist_re, twist_im,
    send_buf, recv_buf, ret_send, ret_recv,
    filt_re, filt_im, cross_buf, part_buf, sum_buf, full_buf,
    send_sem, recv_sem, ret_send_sem, ret_recv_sem, own_sem, load_sem, red_send, red_recv, all_send, all_recv,
):
    me = lax.axis_index("ctx")
    mine = lax.axis_index("dp")
    lines = blocks // cols
    row_at, col_at = lax.div(me, cols), lax.rem(me, cols)
    span = blocks * ROWS
    group = COLS // (2 * ROWS)
    piece = blocks // parts

    line_starts = [lax.rem(row_at + down, lines) * cols for down in range(1, lines + 1)]

    def for_peers(act, first=0, last=cols):
        def turn(step, carry):
            odd = lax.rem(step, 2)
            shift = cols // 2 + lax.div(step + 1, 2) * (1 - 2 * odd)
            column = lax.rem(col_at + shift, cols)
            for start in line_starts:
                act(start + column)
            return carry

        lax.fori_loop(first, min(last, cols - 1), turn, 0)
        if last == cols:
            for start in line_starts[:-1]:
                act(start + col_at)

    def for_parts(act):
        for step in range(1, parts):
            act(lax.rem(mine + step, parts))

    barrier = pltpu.get_barrier_semaphore()
    for_peers(lambda dest: pl.semaphore_signal(barrier, inc=1, device_id={"ctx": dest}, device_id_type=MESH))
    for_parts(lambda dest: pl.semaphore_signal(barrier, inc=1, device_id={"dp": dest}, device_id_type=MESH))

    loads = [
        pltpu.make_async_copy(source, target, load_sem.at[number])
        for number, (source, target) in enumerate(
            (
                (query_hbm, query_ref), (key_hbm, key_ref), (grad_hbm, grad_ref), (value_hbm, value_ref),
                (taps_hbm, taps_ref), (outer_fwd_hbm, outer_fwd), (inner_fwd_hbm, inner_fwd),
                (twist_re_hbm, twist_re), (twist_im_hbm, twist_im),
                (outer_inv_hbm, outer_inv), (inner_inv_hbm, inner_inv),
            )
        )
    ]
    for load in loads:
        load.start()
    for number, (left_ref, right_ref) in enumerate(((query_ref, key_ref), (grad_ref, value_ref))):
        loads[2 * number].wait()
        loads[2 * number + 1].wait()
        for block in range(blocks // group):
            lanes = slice(block * COLS, (block + 1) * COLS)
            product = left_ref[:, lanes].astype(F32) * right_ref[:, lanes].astype(F32)
            turned = product.T.astype(BF16).reshape(group, 2, ROWS, COLS)
            for half in range(2):
                send_buf[half, number, block * group:(block + 1) * group] = turned[:, half]

    pl.semaphore_wait(barrier, blocks - 1 + parts - 1)

    def send_tokens(half):
        def start(dest):
            pltpu.make_async_remote_copy(
                src_ref=send_buf.at[half, :, dest], dst_ref=recv_buf.at[half, :, me],
                send_sem=send_sem.at[half], recv_sem=recv_sem.at[half],
                device_id={"ctx": dest}, device_id_type=MESH,
            ).start()

        for_peers(start)

    def send_back(first, last):
        def start(dest):
            pltpu.make_async_remote_copy(
                src_ref=ret_send.at[:, :, dest], dst_ref=ret_recv.at[:, :, me],
                send_sem=ret_send_sem.at[0], recv_sem=ret_recv_sem.at[0],
                device_id={"ctx": dest}, device_id_type=MESH,
            ).start()

        for_peers(start, first, last)

    def wait_bytes(ref, sem):
        pltpu.make_async_copy(ref, ref, sem).wait()

    def others(ref):
        return ref.at[:, :, pl.ds(0, blocks - 1)]

    def own_copy(half):
        return pltpu.make_async_copy(send_buf.at[half, :, me], recv_buf.at[half, :, me], own_sem.at[half])

    def own_back(half):
        return pltpu.make_async_copy(ret_send.at[half, :, me], ret_recv.at[half, :, me], own_sem.at[2 + half])

    for half in range(2):
        send_tokens(half)
    for half in range(2):
        own_copy(half).start()

    def forward(rows):
        first = dot(outer_fwd[...], rows)
        spectra = []
        for block in range(2):
            lanes = slice(block * COLS, (block + 1) * COLS)
            real, imag = first[:span, lanes], first[span:, lanes]
            turned_re = real * twist_re[...] - imag * twist_im[...]
            turned_im = real * twist_im[...] + imag * twist_re[...]
            both = jnp.concatenate([turned_re.astype(BF16), turned_im.astype(BF16)], axis=1)
            result = dot(both, inner_fwd[...])
            spectra.append((result[:, :COLS], result[:, COLS:]))
        return spectra

    def inverse_inner(real, imag):
        both = jnp.concatenate([real.astype(BF16), imag.astype(BF16)], axis=1)
        result = dot(both, inner_inv[...])
        real, imag = result[:, :COLS], result[:, COLS:]
        turned_re = real * twist_re[...] + imag * twist_im[...]
        turned_im = imag * twist_re[...] - real * twist_im[...]
        return jnp.concatenate([turned_re.astype(BF16), turned_im.astype(BF16)], axis=0)

    for load in loads[4:]:
        load.wait()
    taps_rows = jnp.concatenate(
        [
            jnp.concatenate(
                [taps_ref[half * ROWS:(half + 1) * ROWS, a * COLS:(a + 1) * COLS] for a in range(blocks)], axis=0
            ).astype(BF16)
            for half in range(2)
        ],
        axis=1,
    )
    for half, (real, imag) in enumerate(forward(taps_rows)):
        filt_re[half] = real
        filt_im[half] = imag

    def start_part(half):
        def start(dest):
            pltpu.make_async_remote_copy(
                src_ref=cross_buf.at[half, pl.ds(dest * piece, piece)], dst_ref=part_buf.at[half, mine],
                send_sem=red_send.at[half], recv_sem=red_recv.at[half], device_id={"dp": dest}, device_id_type=MESH,
            ).start()

        for_parts(start)

    def own_part(half):
        return pltpu.make_async_copy(
            cross_buf.at[half, pl.ds(mine * piece, piece)], part_buf.at[half, mine], own_sem.at[4 + half]
        )

    def start_sum(half):
        def start(dest):
            pltpu.make_async_remote_copy(
                src_ref=sum_buf.at[half], dst_ref=full_buf.at[half, mine],
                send_sem=all_send.at[half], recv_sem=all_recv.at[half], device_id={"dp": dest}, device_id_type=MESH,
            ).start()

        for_parts(start)

    def own_sum(half):
        return pltpu.make_async_copy(sum_buf.at[half], full_buf.at[half, mine], own_sem.at[6 + half])

    def add_parts(half):
        wait_bytes(part_buf.at[half, pl.ds(0, parts - 1)], red_recv.at[half])
        own_part(half).wait()
        total = part_buf[half, 0].astype(F32)
        for part in range(1, parts):
            total = total + part_buf[half, part].astype(F32)
        sum_buf[half] = total.astype(BF16)
        start_sum(half)
        own_sum(half).start()

    for half in range(2):
        wait_bytes(recv_buf.at[half, :, pl.ds(0, blocks - 1)], recv_sem.at[half])
        own_copy(half).wait()
        rows = jnp.concatenate(
            [recv_buf[half, 0].reshape(span, COLS), recv_buf[half, 1].reshape(span, COLS)], axis=1
        )
        (gate_re, gate_im), (grad_re, grad_im) = forward(rows)
        cross = inverse_inner(gate_re * grad_re + gate_im * grad_im, gate_re * grad_im - gate_im * grad_re)
        cross_buf[half] = dot(outer_inv[...], cross).astype(BF16).reshape(blocks, ROWS, COLS)
        start_part(half)
        own_part(half).start()
        tap_re, tap_im = filt_re[half], filt_im[half]
        conv = inverse_inner(gate_re * tap_re - gate_im * tap_im, gate_re * tap_im + gate_im * tap_re)
        back = inverse_inner(grad_re * tap_re + grad_im * tap_im, grad_im * tap_re - grad_re * tap_im)
        result = dot(outer_inv[...], jnp.concatenate([conv, back], axis=1)).astype(BF16)
        ret_send[half, 0] = result[:, :COLS].reshape(blocks, ROWS, COLS)
        ret_send[half, 1] = result[:, COLS:].reshape(blocks, ROWS, COLS)
        own_back(half).start()

    send_back(0, cols)
    for half in range(2):
        add_parts(half)
    for half in range(2):
        wait_bytes(full_buf.at[half, pl.ds(0, parts - 1)], all_recv.at[half])
        own_sum(half).wait()
        for a in range(blocks):
            lanes = slice(a * COLS, (a + 1) * COLS)
            filt_out[half * ROWS:(half + 1) * ROWS, lanes] = full_buf[half, a // piece, a % piece]

    wait_bytes(others(ret_recv), ret_recv_sem.at[0])
    for half in range(2):
        own_back(half).wait()
    for number, out_ref in enumerate((conv_out, back_out)):
        for block in range(blocks // group):
            owners = slice(block * group, (block + 1) * group)
            rows = jnp.stack([ret_recv[0, number, owners], ret_recv[1, number, owners]], axis=1)
            out_ref[:, block * COLS:(block + 1) * COLS] = rows.reshape(COLS, COLS).astype(F32).T.astype(BF16)

    for half in range(2):
        wait_bytes(send_buf.at[half, :, pl.ds(0, blocks - 1)], send_sem.at[half])
    wait_bytes(others(ret_send), ret_send_sem.at[0])
    for half in range(2):
        wait_bytes(part_buf.at[half, pl.ds(0, parts - 1)], red_send.at[half])
        wait_bytes(full_buf.at[half, pl.ds(0, parts - 1)], all_send.at[half])


def finish(conv_ref, back_ref, query_ref, key_ref, grad_ref, filt_ref, *rest):
    outs, bufs, sem = rest[:4], rest[4:8], rest[8]
    copies = [pltpu.make_async_copy(buf, out, sem.at[number]) for number, (buf, out) in enumerate(zip(bufs, outs))]
    bufs[3][...] = filt_ref[...].astype(F32)
    copies[3].start()
    back_vals = back_ref[...].astype(F32)
    bufs[0][...] = (back_vals * key_ref[...].astype(F32)).astype(BF16)
    copies[0].start()
    bufs[1][...] = (back_vals * query_ref[...].astype(F32)).astype(BF16)
    copies[1].start()
    bufs[2][...] = (grad_ref[...].astype(F32) * conv_ref[...].astype(F32)).astype(BF16)
    copies[2].start()
    for copy in copies:
        copy.wait()


def local(blocks, parts, cols, query_proj, key_proj, value_proj, out_grad, filter_taps):
    tokens, channels = query_proj.shape[1:]
    tables = make_tables(blocks)
    span = blocks * ROWS
    piece = blocks // parts
    messages = (2, 2, blocks, ROWS, COLS)
    vmem = pl.BlockSpec(memory_space=pltpu.VMEM)
    hbm = pl.BlockSpec(memory_space=pltpu.HBM)
    operands = (query_proj[0], key_proj[0], value_proj[0], out_grad[0], filter_taps, *map(jnp.asarray, tables))
    operands = tuple(pltpu.with_memory_space_constraint(operand, pltpu.HBM) for operand in operands)
    conv_local, back_local, filt_sum = pl.pallas_call(
        functools.partial(kernel, blocks, parts, cols),
        out_shape=(
            jax.ShapeDtypeStruct((tokens, channels), BF16),
            jax.ShapeDtypeStruct((tokens, channels), BF16),
            jax.ShapeDtypeStruct(filter_taps.shape, BF16),
        ),
        in_specs=[hbm] * 11,
        out_specs=(vmem,) * 3,
        scratch_shapes=[
            *(pltpu.VMEM(operand.shape, operand.dtype) for operand in operands),
            pltpu.VMEM(messages, BF16),
            pltpu.VMEM(messages, BF16),
            pltpu.VMEM(messages, BF16),
            pltpu.VMEM(messages, BF16),
            pltpu.VMEM((2, span, COLS), F32),
            pltpu.VMEM((2, span, COLS), F32),
            pltpu.VMEM((2, blocks, ROWS, COLS), BF16),
            pltpu.VMEM((2, parts, piece, ROWS, COLS), BF16),
            pltpu.VMEM((2, piece, ROWS, COLS), BF16),
            pltpu.VMEM((2, parts, piece, ROWS, COLS), BF16),
            pltpu.SemaphoreType.DMA((2,)),
            pltpu.SemaphoreType.DMA((2,)),
            pltpu.SemaphoreType.DMA((2,)),
            pltpu.SemaphoreType.DMA((2,)),
            pltpu.SemaphoreType.DMA((8,)),
            pltpu.SemaphoreType.DMA((11,)),
            pltpu.SemaphoreType.DMA((2,)),
            pltpu.SemaphoreType.DMA((2,)),
            pltpu.SemaphoreType.DMA((2,)),
            pltpu.SemaphoreType.DMA((2,)),
        ],
        compiler_params=pltpu.CompilerParams(
            collective_id=0, has_side_effects=True, vmem_limit_bytes=24 * 2**20
        ),
    )(*operands)
    outs = ((tokens, channels), (tokens, channels), (tokens, channels), filter_taps.shape)
    kinds = (BF16, BF16, BF16, F32)
    grad_q, grad_k, grad_v, grad_filt = pl.pallas_call(
        finish,
        out_shape=tuple(jax.ShapeDtypeStruct(shape, kind) for shape, kind in zip(outs, kinds)),
        in_specs=[vmem] * 6,
        out_specs=(pl.BlockSpec(memory_space=pl.ANY),) * 4,
        scratch_shapes=[
            *(pltpu.VMEM(shape, kind) for shape, kind in zip(outs, kinds)),
            pltpu.SemaphoreType.DMA((4,)),
        ],
        compiler_params=pltpu.CompilerParams(vmem_limit_bytes=8 * 2**20),
    )(conv_local, back_local, query_proj[0], key_proj[0], out_grad[0], filt_sum)
    return grad_q[None], grad_k[None], grad_v[None], grad_filt


def solution(mesh):
    blocks, parts = mesh.shape["ctx"], mesh.shape["dp"]
    cols = max(blocks // 4, 1)
    tokens = P("dp", "ctx", "chan")
    filt = P(("chan", "ctx"), None)
    return jax.shard_map(
        functools.partial(local, blocks, parts, cols),
        mesh=mesh,
        in_specs=(tokens, tokens, tokens, tokens, filt),
        out_specs=(tokens, tokens, tokens, filt),
        check_vma=False,
    )
```

```python
import functools
import math

import jax
import jax.numpy as jnp
import ml_dtypes
import numpy as np
from jax import lax
from jax.experimental import pallas as pl
from jax.experimental.pallas import tpu as pltpu
from jax.sharding import PartitionSpec as P

MESH = pl.DeviceIdType.MESH
ROWS = 16
COLS = 128
F32 = jnp.float32
BF16 = jnp.bfloat16


def make_tables(blocks):
    freq = np.arange(blocks) + 0.5
    outer = np.exp(-2j * np.pi * np.outer(freq, np.arange(blocks)) / (2 * blocks))
    eye = np.eye(ROWS)
    spread = lambda table: np.kron(table, eye)
    outer_fwd = np.concatenate([spread(outer.real), spread(outer.imag)], axis=0)
    length = 2 * blocks * COLS
    back = outer.conj().T * (2.0 / length)
    outer_inv = np.concatenate([spread(back.real), spread(-back.imag)], axis=1)
    inner = np.exp(-2j * np.pi * np.outer(np.arange(COLS), np.arange(COLS)) / COLS)
    inner_fwd = np.block([[inner.real, inner.imag], [-inner.imag, inner.real]])
    inner_inv = np.block([[inner.real, -inner.imag], [inner.imag, inner.real]])
    twist = np.exp(-2j * np.pi * np.outer(freq, np.arange(COLS)) / length)
    twist = np.repeat(twist, ROWS, axis=0)
    half = lambda table: np.asarray(table).astype(ml_dtypes.bfloat16)
    full = lambda table: np.asarray(table).astype(np.float32)
    return (half(outer_fwd), half(outer_inv), half(inner_fwd), half(inner_inv), full(twist.real), full(twist.imag))


def dot(left, right):
    return jnp.dot(left, right, preferred_element_type=F32)


def kernel(
    blocks, parts, cols,
    query_hbm, key_hbm, value_hbm, grad_hbm, taps_hbm,
    outer_fwd_hbm, outer_inv_hbm, inner_fwd_hbm, inner_inv_hbm, twist_re_hbm, twist_im_hbm,
    conv_out, back_out, filt_out,
    query_ref, key_ref, value_ref, grad_ref, taps_ref,
    outer_fwd, outer_inv, inner_fwd, inner_inv, twist_re, twist_im,
    send_buf, recv_buf, ret_send, ret_recv,
    filt_re, filt_im, cross_buf, part_buf, sum_buf, full_buf,
    send_sem, recv_sem, ret_send_sem, ret_recv_sem, own_sem, load_sem, red_send, red_recv, all_send, all_recv,
):
    me = lax.axis_index("ctx")
    mine = lax.axis_index("dp")
    lines = blocks // cols
    row_at, col_at = lax.div(me, cols), lax.rem(me, cols)
    span = blocks * ROWS
    group = COLS // (2 * ROWS)
    piece = blocks // parts

    line_starts = [lax.rem(row_at + down, lines) * cols for down in range(1, lines + 1)]

    def for_peers(act, first=0, last=cols):
        def turn(step, carry):
            odd = lax.rem(step, 2)
            shift = cols // 2 + lax.div(step + 1, 2) * (1 - 2 * odd)
            column = lax.rem(col_at + shift, cols)
            for start in line_starts:
                act(start + column)
            return carry

        lax.fori_loop(first, min(last, cols - 1), turn, 0)
        if first < last == cols:
            for start in line_starts[:-1]:
                act(start + col_at)

    def for_parts(act):
        for step in range(1, parts):
            act(lax.rem(mine + step, parts))

    barrier = pltpu.get_barrier_semaphore()
    for_peers(lambda dest: pl.semaphore_signal(barrier, inc=1, device_id={"ctx": dest}, device_id_type=MESH))
    for_parts(lambda dest: pl.semaphore_signal(barrier, inc=1, device_id={"dp": dest}, device_id_type=MESH))

    loads = [
        pltpu.make_async_copy(source, target, load_sem.at[number])
        for number, (source, target) in enumerate(
            (
                (query_hbm, query_ref), (key_hbm, key_ref), (grad_hbm, grad_ref), (value_hbm, value_ref),
                (taps_hbm, taps_ref), (outer_fwd_hbm, outer_fwd), (inner_fwd_hbm, inner_fwd),
                (twist_re_hbm, twist_re), (twist_im_hbm, twist_im),
                (outer_inv_hbm, outer_inv), (inner_inv_hbm, inner_inv),
            )
        )
    ]
    for load in loads:
        load.start()
    for number, (left_ref, right_ref) in enumerate(((query_ref, key_ref), (grad_ref, value_ref))):
        loads[2 * number].wait()
        loads[2 * number + 1].wait()
        for block in range(blocks // group):
            lanes = slice(block * COLS, (block + 1) * COLS)
            product = left_ref[:, lanes].astype(F32) * right_ref[:, lanes].astype(F32)
            turned = product.T.astype(BF16).reshape(group, 2, ROWS, COLS)
            for half in range(2):
                send_buf[half, number, block * group:(block + 1) * group] = turned[:, half]

    pl.semaphore_wait(barrier, blocks - 1 + parts - 1)

    def send_tokens(half):
        def start(dest):
            pltpu.make_async_remote_copy(
                src_ref=send_buf.at[half, :, dest], dst_ref=recv_buf.at[half, :, me],
                send_sem=send_sem.at[half], recv_sem=recv_sem.at[half],
                device_id={"ctx": dest}, device_id_type=MESH,
            ).start()

        for_peers(start)

    def send_back(first, last):
        def start(dest):
            pltpu.make_async_remote_copy(
                src_ref=ret_send.at[:, :, dest], dst_ref=ret_recv.at[:, :, me],
                send_sem=ret_send_sem.at[0], recv_sem=ret_recv_sem.at[0],
                device_id={"ctx": dest}, device_id_type=MESH,
            ).start()

        for_peers(start, first, last)

    def wait_bytes(ref, sem):
        pltpu.make_async_copy(ref, ref, sem).wait()

    def others(ref):
        return ref.at[:, :, pl.ds(0, blocks - 1)]

    def own_copy(half):
        return pltpu.make_async_copy(send_buf.at[half, :, me], recv_buf.at[half, :, me], own_sem.at[half])

    def own_back(half):
        return pltpu.make_async_copy(ret_send.at[half, :, me], ret_recv.at[half, :, me], own_sem.at[2 + half])

    for half in range(2):
        send_tokens(half)
    for half in range(2):
        own_copy(half).start()

    def forward(rows):
        first = dot(outer_fwd[...], rows)
        spectra = []
        for block in range(2):
            lanes = slice(block * COLS, (block + 1) * COLS)
            real, imag = first[:span, lanes], first[span:, lanes]
            turned_re = real * twist_re[...] - imag * twist_im[...]
            turned_im = real * twist_im[...] + imag * twist_re[...]
            both = jnp.concatenate([turned_re.astype(BF16), turned_im.astype(BF16)], axis=1)
            result = dot(both, inner_fwd[...])
            spectra.append((result[:, :COLS], result[:, COLS:]))
        return spectra

    def inverse_inner(real, imag):
        both = jnp.concatenate([real.astype(BF16), imag.astype(BF16)], axis=1)
        result = dot(both, inner_inv[...])
        real, imag = result[:, :COLS], result[:, COLS:]
        turned_re = real * twist_re[...] + imag * twist_im[...]
        turned_im = imag * twist_re[...] - real * twist_im[...]
        return jnp.concatenate([turned_re.astype(BF16), turned_im.astype(BF16)], axis=0)

    for load in loads[4:]:
        load.wait()
    taps_rows = jnp.concatenate(
        [
            jnp.concatenate(
                [taps_ref[half * ROWS:(half + 1) * ROWS, a * COLS:(a + 1) * COLS] for a in range(blocks)], axis=0
            ).astype(BF16)
            for half in range(2)
        ],
        axis=1,
    )
    for half, (real, imag) in enumerate(forward(taps_rows)):
        filt_re[half] = real
        filt_im[half] = imag

    def start_part(half):
        def start(dest):
            pltpu.make_async_remote_copy(
                src_ref=cross_buf.at[half, pl.ds(dest * piece, piece)], dst_ref=part_buf.at[half, mine],
                send_sem=red_send.at[half], recv_sem=red_recv.at[half], device_id={"dp": dest}, device_id_type=MESH,
            ).start()

        for_parts(start)

    def own_part(half):
        return pltpu.make_async_copy(
            cross_buf.at[half, pl.ds(mine * piece, piece)], part_buf.at[half, mine], own_sem.at[4 + half]
        )

    def start_sum(half):
        def start(dest):
            pltpu.make_async_remote_copy(
                src_ref=sum_buf.at[half], dst_ref=full_buf.at[half, mine],
                send_sem=all_send.at[half], recv_sem=all_recv.at[half], device_id={"dp": dest}, device_id_type=MESH,
            ).start()

        for_parts(start)

    def own_sum(half):
        return pltpu.make_async_copy(sum_buf.at[half], full_buf.at[half, mine], own_sem.at[6 + half])

    def add_parts(half):
        wait_bytes(part_buf.at[half, pl.ds(0, parts - 1)], red_recv.at[half])
        own_part(half).wait()
        total = part_buf[half, 0].astype(F32)
        for part in range(1, parts):
            total = total + part_buf[half, part].astype(F32)
        sum_buf[half] = total.astype(BF16)
        start_sum(half)
        own_sum(half).start()

    for half in range(2):
        wait_bytes(recv_buf.at[half, :, pl.ds(0, blocks - 1)], recv_sem.at[half])
        own_copy(half).wait()
        rows = jnp.concatenate(
            [recv_buf[half, 0].reshape(span, COLS), recv_buf[half, 1].reshape(span, COLS)], axis=1
        )
        (gate_re, gate_im), (grad_re, grad_im) = forward(rows)
        if half == 0:
            cross = inverse_inner(gate_re * grad_re + gate_im * grad_im, gate_re * grad_im - gate_im * grad_re)
            cross_buf[half] = dot(outer_inv[...], cross).astype(BF16).reshape(blocks, ROWS, COLS)
            start_part(half)
            own_part(half).start()
        tap_re, tap_im = filt_re[half], filt_im[half]
        conv = inverse_inner(gate_re * tap_re - gate_im * tap_im, gate_re * tap_im + gate_im * tap_re)
        back = inverse_inner(grad_re * tap_re + grad_im * tap_im, grad_im * tap_re - grad_re * tap_im)
        result = dot(outer_inv[...], jnp.concatenate([conv, back], axis=1)).astype(BF16)
        ret_send[half, 0] = result[:, :COLS].reshape(blocks, ROWS, COLS)
        ret_send[half, 1] = result[:, COLS:].reshape(blocks, ROWS, COLS)
        own_back(half).start()
        if half == 1:
            send_back(0, 1)
            cross = inverse_inner(gate_re * grad_re + gate_im * grad_im, gate_re * grad_im - gate_im * grad_re)
            cross_buf[half] = dot(outer_inv[...], cross).astype(BF16).reshape(blocks, ROWS, COLS)
            start_part(half)
            own_part(half).start()

    send_back(1, cols)
    for half in range(2):
        add_parts(half)
    for half in range(2):
        wait_bytes(full_buf.at[half, pl.ds(0, parts - 1)], all_recv.at[half])
        own_sum(half).wait()
        for a in range(blocks):
            lanes = slice(a * COLS, (a + 1) * COLS)
            filt_out[half * ROWS:(half + 1) * ROWS, lanes] = full_buf[half, a // piece, a % piece]

    wait_bytes(others(ret_recv), ret_recv_sem.at[0])
    for half in range(2):
        own_back(half).wait()
    for number, out_ref in enumerate((conv_out, back_out)):
        for block in range(blocks // group):
            owners = slice(block * group, (block + 1) * group)
            rows = jnp.stack([ret_recv[0, number, owners], ret_recv[1, number, owners]], axis=1)
            out_ref[:, block * COLS:(block + 1) * COLS] = rows.reshape(COLS, COLS).astype(F32).T.astype(BF16)

    for half in range(2):
        wait_bytes(send_buf.at[half, :, pl.ds(0, blocks - 1)], send_sem.at[half])
    wait_bytes(others(ret_send), ret_send_sem.at[0])
    for half in range(2):
        wait_bytes(part_buf.at[half, pl.ds(0, parts - 1)], red_send.at[half])
        wait_bytes(full_buf.at[half, pl.ds(0, parts - 1)], all_send.at[half])


def finish(conv_ref, back_ref, query_ref, key_ref, grad_ref, filt_ref, *rest):
    outs, bufs, sem = rest[:4], rest[4:8], rest[8]
    copies = [pltpu.make_async_copy(buf, out, sem.at[number]) for number, (buf, out) in enumerate(zip(bufs, outs))]
    bufs[3][...] = filt_ref[...].astype(F32)
    copies[3].start()
    back_vals = back_ref[...].astype(F32)
    bufs[0][...] = (back_vals * key_ref[...].astype(F32)).astype(BF16)
    copies[0].start()
    bufs[1][...] = (back_vals * query_ref[...].astype(F32)).astype(BF16)
    copies[1].start()
    bufs[2][...] = (grad_ref[...].astype(F32) * conv_ref[...].astype(F32)).astype(BF16)
    copies[2].start()
    for copy in copies:
        copy.wait()


def local(blocks, parts, cols, query_proj, key_proj, value_proj, out_grad, filter_taps):
    tokens, channels = query_proj.shape[1:]
    tables = make_tables(blocks)
    span = blocks * ROWS
    piece = blocks // parts
    messages = (2, 2, blocks, ROWS, COLS)
    vmem = pl.BlockSpec(memory_space=pltpu.VMEM)
    hbm = pl.BlockSpec(memory_space=pltpu.HBM)
    operands = (query_proj[0], key_proj[0], value_proj[0], out_grad[0], filter_taps, *map(jnp.asarray, tables))
    operands = tuple(pltpu.with_memory_space_constraint(operand, pltpu.HBM) for operand in operands)
    conv_local, back_local, filt_sum = pl.pallas_call(
        functools.partial(kernel, blocks, parts, cols),
        out_shape=(
            jax.ShapeDtypeStruct((tokens, channels), BF16),
            jax.ShapeDtypeStruct((tokens, channels), BF16),
            jax.ShapeDtypeStruct(filter_taps.shape, BF16),
        ),
        in_specs=[hbm] * 11,
        out_specs=(vmem,) * 3,
        scratch_shapes=[
            *(pltpu.VMEM(operand.shape, operand.dtype) for operand in operands),
            pltpu.VMEM(messages, BF16),
            pltpu.VMEM(messages, BF16),
            pltpu.VMEM(messages, BF16),
            pltpu.VMEM(messages, BF16),
            pltpu.VMEM((2, span, COLS), F32),
            pltpu.VMEM((2, span, COLS), F32),
            pltpu.VMEM((2, blocks, ROWS, COLS), BF16),
            pltpu.VMEM((2, parts, piece, ROWS, COLS), BF16),
            pltpu.VMEM((2, piece, ROWS, COLS), BF16),
            pltpu.VMEM((2, parts, piece, ROWS, COLS), BF16),
            pltpu.SemaphoreType.DMA((2,)),
            pltpu.SemaphoreType.DMA((2,)),
            pltpu.SemaphoreType.DMA((2,)),
            pltpu.SemaphoreType.DMA((2,)),
            pltpu.SemaphoreType.DMA((8,)),
            pltpu.SemaphoreType.DMA((11,)),
            pltpu.SemaphoreType.DMA((2,)),
            pltpu.SemaphoreType.DMA((2,)),
            pltpu.SemaphoreType.DMA((2,)),
            pltpu.SemaphoreType.DMA((2,)),
        ],
        compiler_params=pltpu.CompilerParams(
            collective_id=0, has_side_effects=True, vmem_limit_bytes=24 * 2**20
        ),
    )(*operands)
    outs = ((tokens, channels), (tokens, channels), (tokens, channels), filter_taps.shape)
    kinds = (BF16, BF16, BF16, F32)
    grad_q, grad_k, grad_v, grad_filt = pl.pallas_call(
        finish,
        out_shape=tuple(jax.ShapeDtypeStruct(shape, kind) for shape, kind in zip(outs, kinds)),
        in_specs=[vmem] * 6,
        out_specs=(pl.BlockSpec(memory_space=pl.ANY),) * 4,
        scratch_shapes=[
            *(pltpu.VMEM(shape, kind) for shape, kind in zip(outs, kinds)),
            pltpu.SemaphoreType.DMA((4,)),
        ],
        compiler_params=pltpu.CompilerParams(vmem_limit_bytes=8 * 2**20),
    )(conv_local, back_local, query_proj[0], key_proj[0], out_grad[0], filt_sum)
    return grad_q[None], grad_k[None], grad_v[None], grad_filt


def solution(mesh):
    blocks, parts = mesh.shape["ctx"], mesh.shape["dp"]
    cols = max(blocks // 4, 1)
    tokens = P("dp", "ctx", "chan")
    filt = P(("chan", "ctx"), None)
    return jax.shard_map(
        functools.partial(local, blocks, parts, cols),
        mesh=mesh,
        in_specs=(tokens, tokens, tokens, tokens, filt),
        out_specs=(tokens, tokens, tokens, filt),
        check_vma=False,
    )
```
